512 devices in a mesh: row: 32 (over y, z_hi, core), col: 16 (over z_lo, x).
Axes of the slice: x: 4, y: 4, z: 16 (z_hi: 4, z_lo: 4; z = z_hi * 4 + z_lo), core: 2. Of those that a mesh axis runs over, the one named last changes fastest.
Arguments:
- forcing_terms: float32 [32, 16, 2, 32, 128], P('row', 'col'), may hold values from -6 to 6
- diagonal_reciprocal: float32 [32, 16, 2, 128, 128], P('row', 'col'), may hold values from -0.5 to 0.5
- stiffness_submatrix: float32 [32, 16, 32, 128, 128], P('row', 'col'), may hold values from -0.1875 to 0.1875
- stiffness_source_index: int32 [32, 16, 32], P('row', 'col'), may hold values from 0 to 31
- stiffness_target_index: int32 [32, 16, 32], P('row', 'col'), may hold values from 0 to 63
- stiffness_nonzero_tally: int32 [32, 16], P('row', 'col'), may hold values from 1 to 32, as said below
- interpolant_submatrix: float32 [32, 16, 16, 128, 128], P('row', 'col'), may hold values from -0.0625 to 0.0625
- interpolant_cluster_index: int32 [32, 16, 16], P('row', 'col'), may hold values from 0 to 1
- interpolant_target_index: int32 [32, 16, 16], P('row', 'col'), may hold values from 0 to 63
- interpolant_nonzero_tally: int32 [32, 16], P('row', 'col'), may hold values from 1 to 16, as said below
- provisional_interpolant: float32 [32, 16, 2, 128], P('row', 'col'), may hold values from 0.2 to 1
- cluster_label: int32 [32, 16, 2, 128], P('row', 'col'), may hold values from 0 to 255
Outputs:
- relaxed_iterate: float32 [32, 16, 2, 32, 128], P('row', 'col')
- residual: float32 [32, 16, 2, 32, 128], P('row', 'col')
- coarse: float32 [32, 2, 32, 128], P('row')
The draws below stay inside these ranges and needn't reach their ends.
Inputs may be any that keep to these rules, and one draw needn't show every extreme that they name: `stiffness_nonzero_tally`: tile slots at or past the count are unused; some pair has all 32 slots live in every draw. `interpolant_nonzero_tally`: tile slots at or past the count are unused; some pair has all 16 slots live in every draw.
All inputs are finite; a program needn't handle non-finite values.
Results may differ from the reference program's by a relative error of at most 0.0003.
Values sent between devices are 32-bit elements; how exact they have to be, the bound alone decides.
No kernel may reach another device: no remote copies, remote signals or barrier semaphores. Data moves between devices by JAX's collectives and lax.ppermute only.
A program may use at most 64 MiB of HBM per device.

```python
import jax
import jax.numpy as jnp
from jax import lax

TILE_ORDER_SIZE = 128
PB = 2
RHS = 32
BAND_COUNT = 32
BAND_MEMBERS = 16
PAIR_CAPACITY = 32
PSLOT = 16


def skewed_counts(key, most):
    first_key = jax.random.fold_in(key, 5)
    second_key = jax.random.fold_in(key, 9)
    base = jax.random.randint(first_key, (BAND_COUNT * BAND_MEMBERS,), 1, most + 1)
    chosen = jax.random.randint(second_key, (), 0, BAND_COUNT * BAND_MEMBERS)
    filled = jnp.where(jnp.arange(BAND_COUNT * BAND_MEMBERS) == chosen, most, base)
    return filled.reshape(BAND_COUNT, BAND_MEMBERS).astype(jnp.int32)


def draw_stiffness_nonzero_tally(key, part):
    return skewed_counts(jax.random.fold_in(key, 11), PAIR_CAPACITY)


def draw_interpolant_nonzero_tally(key, part):
    return skewed_counts(jax.random.fold_in(key, 23), PSLOT)


def place_ends(drawn, rng, low, high):
    extent = drawn.shape
    index_at = [jax.random.randint(jax.random.fold_in(rng, axis), (), 0, extent[axis]) for axis in range(len(extent))]
    drawn = drawn.at[tuple(index_at)].set(low)
    longest = extent.index(max(extent))
    index_at[longest] = (index_at[longest] + 1) % extent[longest]
    return drawn.at[tuple(index_at)].set(high)


def shard_levels(rng, dims, shards, least, high):
    loudness, own = 1.0, jax.random.fold_in(rng, 6)
    for position, shards_of in shards:
        steps = jnp.exp(jax.random.uniform(jax.random.fold_in(own, position), (shards_of,), jnp.float32, least / len(shards), high / len(shards)))
        loudness = loudness * jnp.repeat(steps, dims[position] // shards_of).reshape([-1 if axis == position else 1 for axis in range(len(dims))])
    return loudness


def centred(stream_key, shape, width, limit, split=(), held_as=jnp.bfloat16):
    drawn = width * jax.random.normal(stream_key, shape, jnp.float32)
    if split:
        drawn = drawn * shard_levels(stream_key, shape, split, -0.22, 0.18)
    return jnp.clip(drawn, -limit, limit).astype(held_as)


def setup_inputs(seed: int = 0) -> dict:
    keys = jax.random.split(jax.random.key(seed), 13)
    return {
        "forcing_terms": centred(keys[0], (BAND_COUNT, BAND_MEMBERS, PB, RHS, TILE_ORDER_SIZE), 1.0, 6.0, ((0, 32), (1, 16)), jnp.float32),
        "diagonal_reciprocal": centred(keys[1], (BAND_COUNT, BAND_MEMBERS, PB, TILE_ORDER_SIZE, TILE_ORDER_SIZE), TILE_ORDER_SIZE ** -0.5, 0.5, ((0, 32), (1, 16)), jnp.float32),
        "stiffness_submatrix": centred(keys[2], (BAND_COUNT, BAND_MEMBERS, PAIR_CAPACITY, TILE_ORDER_SIZE, TILE_ORDER_SIZE), (TILE_ORDER_SIZE * 8) ** -0.5, 0.1875, ((0, 32), (1, 16)), jnp.float32),
        "stiffness_source_index": place_ends(jax.random.randint(keys[3], (BAND_COUNT, BAND_MEMBERS, PAIR_CAPACITY), 0, BAND_MEMBERS * PB), jax.random.fold_in(keys[3], 1), 0, (BAND_MEMBERS * PB) - 1).astype(jnp.int32),
        "stiffness_target_index": place_ends(jax.random.randint(keys[4], (BAND_COUNT, BAND_MEMBERS, PAIR_CAPACITY), 0, BAND_COUNT * PB), jax.random.fold_in(keys[4], 1), 0, (BAND_COUNT * PB) - 1).astype(jnp.int32),
        "stiffness_nonzero_tally": draw_stiffness_nonzero_tally(jax.random.fold_in(keys[12], 71), 0),
        "interpolant_submatrix": centred(keys[6], (BAND_COUNT, BAND_MEMBERS, PSLOT, TILE_ORDER_SIZE, TILE_ORDER_SIZE), (TILE_ORDER_SIZE * 4 * BAND_MEMBERS) ** -0.5, 0.0625, ((0, 32), (1, 16)), jnp.float32),
        "interpolant_cluster_index": place_ends(jax.random.randint(keys[7], (BAND_COUNT, BAND_MEMBERS, PSLOT), 0, PB), jax.random.fold_in(keys[7], 1), 0, PB - 1).astype(jnp.int32),
        "interpolant_target_index": place_ends(jax.random.randint(keys[8], (BAND_COUNT, BAND_MEMBERS, PSLOT), 0, BAND_COUNT * PB), jax.random.fold_in(keys[8], 1), 0, (BAND_COUNT * PB) - 1).astype(jnp.int32),
        "interpolant_nonzero_tally": draw_interpolant_nonzero_tally(jax.random.fold_in(keys[12], 71), 0),
        "provisional_interpolant": jnp.clip(0.2 + 0.8 * jax.random.uniform(keys[10], (BAND_COUNT, BAND_MEMBERS, PB, TILE_ORDER_SIZE), jnp.float32) ** shard_levels(keys[10], (BAND_COUNT, BAND_MEMBERS, PB, TILE_ORDER_SIZE), ((0, 32), (1, 16)), -0.2, 0.2), 0.2, 1.0),
        "cluster_label": place_ends(jax.random.randint(keys[11], (BAND_COUNT, BAND_MEMBERS, PB, TILE_ORDER_SIZE), 0, PB * TILE_ORDER_SIZE), jax.random.fold_in(keys[11], 1), 0, (PB * TILE_ORDER_SIZE) - 1).astype(jnp.int32),
    }


omega = 0.7
highest = lax.Precision.HIGHEST


def tile_terms(blocks, stiffness_submatrices, rows, cols, count, nout):
    inputs = jnp.take(blocks, cols, axis=0)
    product = jnp.einsum('ska,sab->skb', inputs, stiffness_submatrices, precision=highest)
    live = (jnp.arange(stiffness_submatrices.shape[0]) < count).astype(jnp.float32)
    onehot = (rows[:, None] == jnp.arange(nout)[None, :]).astype(jnp.float32) * live[:, None]
    return jnp.einsum('so,skb->okb', onehot, product, precision=highest)


def precondition(vec, diagonal_reciprocal):
    return jnp.einsum('ijpka,ijpab->ijpkb', vec, diagonal_reciprocal, precision=highest)


def stiffness_product(vec, stiffness_submatrices, rows, cols, counts):
    nrg, ncg, pb, nrhs, blk = vec.shape

    def one_row(args):
        tile_row, row_ids, col_ids, count_row = args

        def one_col(index, tiles_one, rows_one, cols_one, count_one):
            blocks = jnp.take(vec, index, axis=1).reshape(nrg * pb, nrhs, blk)
            return tile_terms(blocks, tiles_one, rows_one, cols_one, count_one, ncg * pb)

        terms = jax.vmap(one_col)(jnp.arange(ncg), tile_row, row_ids, col_ids, count_row)
        return jnp.sum(terms, axis=0).reshape(ncg, pb, nrhs, blk)

    return lax.map(one_row, (stiffness_submatrices, rows, cols, counts))


def restrict(residual, interpolant_submatrix, interpolant_cluster_index, interpolant_target_index, interpolant_nonzero_tally, provisional_interpolant, cluster_label):
    nrg, ncg, pb, nrhs, blk = residual.shape

    def one_row(args):
        tile_row, row_ids, col_ids, count_row, tent_row, agg_row, resid_row = args

        def one_col(index, tiles_one, rows_one, cols_one, count_one, tent_one, agg_one, resid_one):
            blocks = jnp.take(residual, index, axis=1).reshape(nrg * pb, nrhs, blk)
            part = tile_terms(blocks, tiles_one, rows_one, cols_one, count_one, pb)
            weighted = (resid_one * tent_one[:, None, :]).transpose(1, 0, 2).reshape(nrhs, pb * blk)
            onehot = (agg_one.reshape(-1)[:, None] == jnp.arange(pb * blk)[None, :]).astype(jnp.float32)
            tentative = jnp.dot(weighted, onehot, precision=highest)
            return part + tentative.reshape(nrhs, pb, blk).transpose(1, 0, 2)

        terms = jax.vmap(one_col)(jnp.arange(ncg), tile_row, row_ids, col_ids, count_row, tent_row, agg_row, resid_row)
        return jnp.sum(terms, axis=0)

    return lax.map(one_row, (interpolant_submatrix, interpolant_cluster_index, interpolant_target_index, interpolant_nonzero_tally, provisional_interpolant, cluster_label, residual))


def reference(forcing_terms, diagonal_reciprocal, stiffness_submatrix, stiffness_source_index, stiffness_target_index, stiffness_nonzero_tally, interpolant_submatrix, interpolant_cluster_index, interpolant_target_index, interpolant_nonzero_tally, provisional_interpolant, cluster_label):
    starting_guess = omega * precondition(forcing_terms, diagonal_reciprocal)
    image_field = stiffness_product(starting_guess, stiffness_submatrix, stiffness_source_index, stiffness_target_index, stiffness_nonzero_tally)
    relaxed_iterate = starting_guess + omega * precondition(forcing_terms - image_field, diagonal_reciprocal)
    image_field = stiffness_product(relaxed_iterate, stiffness_submatrix, stiffness_source_index, stiffness_target_index, stiffness_nonzero_tally)
    residual = forcing_terms - image_field
    coarse = restrict(residual, interpolant_submatrix, interpolant_cluster_index, interpolant_target_index, interpolant_nonzero_tally, provisional_interpolant, cluster_label)
    return relaxed_iterate, residual, coarse
```

```python
import functools

import jax
import jax.numpy as jnp
from jax import lax
from jax.experimental import pallas as pl
from jax.experimental.pallas import tpu as pltpu
from jax.sharding import Mesh, PartitionSpec as P

omega = 0.7
unroll = 4
f32 = jnp.float32
bf16 = jnp.bfloat16


def split(v):
    high = v.astype(bf16)
    return high, (v - high.astype(f32)).astype(bf16)


def product(x, w):
    n, m = x.shape[0], w.shape[1]
    left = jnp.concatenate(split(x), axis=0)
    right = jnp.concatenate(split(w), axis=1)
    full = jnp.dot(left, right, preferred_element_type=f32)
    small = full[:n, m:] + full[n:, :m] + full[n:, m:]
    return full[:n, :m] + small


def spread(ref, value, p):
    for copy in range(ref.shape[0]):
        ref[copy, p] = value


def first_kernel(source, inverse, first, copies):
    for p in range(source.shape[0]):
        value = omega * product(source[p], inverse[p])
        first[p] = value
        spread(copies, value, p)


def column_sum(parts, p):
    total = parts[0, p]
    for j in range(1, parts.shape[0]):
        total = total + parts[j, p]
    return total


def relax_kernel(source, inverse, first, parts, relaxed, copies):
    for p in range(source.shape[0]):
        image = column_sum(parts, p)
        value = first[p] + omega * product(source[p] - image, inverse[p])
        relaxed[p] = value
        spread(copies, value, p)


def residual_kernel(source, parts, weights, labels, residual, copies, tentative):
    pblocks, nrhs, width = source.shape
    total = jnp.zeros((nrhs, pblocks * width), f32)
    for p in range(pblocks):
        value = source[p] - column_sum(parts, p)
        residual[p] = value
        spread(copies, value, p)
        weighted = value * weights[p : p + 1, :]
        aggregate = lax.broadcasted_iota(jnp.int32, (pblocks * width, width), 0)
        member = (aggregate == labels[p : p + 1, :]).astype(f32).astype(bf16)
        high, rest = split(weighted)
        low = (weighted - high.astype(f32) - rest.astype(f32)).astype(bf16)
        stacked = jnp.concatenate([high, rest, low, low], axis=0)
        spreadsum = lax.dot_general(
            stacked, member, (((1,), (1,)), ((), ())), preferred_element_type=f32
        )
        total = total + (
            spreadsum[:nrhs]
            + (spreadsum[nrhs : 2 * nrhs] + spreadsum[2 * nrhs : 3 * nrhs])
        )
    for p in range(pblocks):
        tentative[p] = total[:, p * width : (p + 1) * width]


def sum_kernel(parts, out):
    for p in range(out.shape[0]):
        out[p] = column_sum(parts, p)


def tile_kernel(core, count, rows, cols, own, other, tiles, start, out):
    nout = out.shape[0]
    nsource = own.shape[0]
    capacity = tiles.shape[0]
    live_count = count[0]
    mine = core[0]
    if start is None:
        out[...] = jnp.zeros_like(out)
    else:
        out[...] = start[...]

    def group(g, carry):
        terms = []
        for u in range(unroll):
            slot = g * unroll + u
            live = slot < live_count
            target = jnp.clip(cols[slot], 0, 2 * nsource - 1)
            index = (target // 4) * 2 + target % 2
            same = (target // 2) % 2 == mine
            x = jnp.where(same, own[index], other[index])
            x = jnp.where(live, x, 0.0)
            terms.append((jnp.clip(rows[slot], 0, nout - 1), product(x, tiles[slot])))
        for row, term in terms:
            out[row] = out[row] + term
        return carry

    lax.fori_loop(0, (live_count + unroll - 1) // unroll, group, 0)


def vmem(n):
    return [pl.BlockSpec(memory_space=pltpu.VMEM)] * n


def smem(n):
    return [pl.BlockSpec(memory_space=pltpu.SMEM)] * n


def call(kernel, name, shapes, *args):
    return pl.pallas_call(
        kernel,
        out_shape=tuple(jax.ShapeDtypeStruct(s, f32) for s in shapes),
        in_specs=vmem(len(args)),
        out_specs=tuple(vmem(len(shapes))),
        name=name,
    )(*args)


def tile_terms(name, core, count, rows, cols, own, other, tiles, start, nout):
    block = own.shape[1:]
    extra = () if start is None else (start,)

    def kernel(core, count, rows, cols, own, other, tiles, *rest):
        tile_kernel(core, count, rows, cols, own, other, tiles,
                    None if start is None else rest[0], rest[-1])

    return pl.pallas_call(
        kernel,
        out_shape=jax.ShapeDtypeStruct((nout,) + block, f32),
        in_specs=smem(4) + vmem(3 + len(extra)),
        out_specs=pl.BlockSpec(memory_space=pltpu.VMEM),
        name=name,
    )(core, count, rows, cols, own, other, tiles, *extra)


def gather_rows(copies):
    nz, ny = lax.axis_size("zh"), lax.axis_size("y")
    block = copies.shape[2:]
    planes = lax.all_to_all(copies, "zh", 0, 0, tiled=True)
    slab = lax.optimization_barrier(
        jnp.broadcast_to(planes[None], (ny,) + planes.shape)
    )
    own = lax.all_to_all(slab, "y", 0, 0, tiled=True).reshape((-1,) + block)
    other = lax.ppermute(own, "core", [(0, 1), (1, 0)])
    return own, other


def sum_columns(partial, pblocks):
    chunks = partial.reshape((-1, pblocks) + partial.shape[1:])
    return lax.all_to_all(chunks, ("zl", "x"), 0, 0, tiled=True)


def body(
    forcing_terms,
    diagonal_reciprocal,
    stiffness_submatrix,
    stiffness_source_index,
    stiffness_target_index,
    stiffness_nonzero_tally,
    interpolant_submatrix,
    interpolant_cluster_index,
    interpolant_target_index,
    interpolant_nonzero_tally,
    provisional_interpolant,
    cluster_label,
):
    source = forcing_terms[0, 0]
    inverse = diagonal_reciprocal[0, 0]
    tiles = stiffness_submatrix[0, 0]
    rows = stiffness_source_index[0, 0]
    cols = stiffness_target_index[0, 0]
    count = stiffness_nonzero_tally[0]
    core = lax.axis_index("core").astype(jnp.int32).reshape(1)
    pblocks = source.shape[0]
    ncol = lax.axis_size(("zl", "x"))
    nz = lax.axis_size("zh")
    block = source.shape
    spreads = (nz,) + block

    first, copies = call(first_kernel, "first", (block, spreads), source, inverse)
    own, other = gather_rows(copies)
    partial = tile_terms("image1", core, count, rows, cols, own, other, tiles, None, ncol * pblocks)
    parts = sum_columns(partial, pblocks)
    relaxed, copies = call(
        relax_kernel, "relax", (block, spreads), source, inverse, first, parts
    )
    own, other = gather_rows(copies)
    partial = tile_terms("image2", core, count, rows, cols, own, other, tiles, None, ncol * pblocks)
    parts = sum_columns(partial, pblocks)
    residual, copies, tentative = call(
        residual_kernel,
        "residual",
        (block, spreads, block),
        source,
        parts,
        provisional_interpolant[0, 0],
        cluster_label[0, 0],
    )
    own, other = gather_rows(copies)
    share = tile_terms(
        "restrict",
        core,
        interpolant_nonzero_tally[0],
        interpolant_cluster_index[0, 0],
        interpolant_target_index[0, 0],
        own,
        other,
        interpolant_submatrix[0, 0],
        tentative,
        pblocks,
    )
    shares = lax.optimization_barrier(jnp.broadcast_to(share[None], (ncol,) + block))
    shares = lax.all_to_all(shares, ("zl", "x"), 0, 0, tiled=True)
    (coarse,) = call(sum_kernel, "coarse", (block,), shares)
    return (relaxed[None, None], residual[None, None], coarse[None])


def solution(mesh):
    grid = Mesh(mesh.devices.reshape(4, 4, 2, 4, 4), ("y", "zh", "core", "zl", "x"))
    row = ("y", "zh", "core")
    col = ("zl", "x")
    spec = P(row, col)
    return jax.shard_map(
        body,
        mesh=grid,
        in_specs=(spec,) * 12,
        out_specs=(spec, spec, P(row)),
        check_vma=False,
    )
```

```python
import jax
import jax.numpy as jnp
from jax import lax
from jax.experimental import pallas as pl
from jax.experimental.pallas import tpu as pltpu
from jax.sharding import Mesh, PartitionSpec as P


omega = 0.7
unroll = 16
grant = 16 * 2**20
f32 = jnp.float32
bf16 = jnp.bfloat16


def split(v):
    high = v.astype(bf16)
    return high, (v - high.astype(f32)).astype(bf16)


def product(x, w):
    n, m = x.shape[0], w.shape[1]
    left = jnp.concatenate(split(x), axis=0)
    right = jnp.concatenate(split(w), axis=1)
    full = jnp.dot(left, right, preferred_element_type=f32)
    small = full[:n, m:] + full[n:, :m] + full[n:, m:]
    return full[:n, :m] + small


def first_kernel(source_in, inverse_in, first, source, inverse, done):
    arrivals = [
        pltpu.make_async_copy(inverse_in, inverse, done.at[0]),
        pltpu.make_async_copy(source_in, source, done.at[1]),
    ]
    for arrival in arrivals:
        arrival.start()
    for arrival in arrivals:
        arrival.wait()
    for p in range(source.shape[0]):
        first[p] = omega * product(source[p], inverse[p])


def column_sum(parts, p):
    total = parts[0, p]
    for j in range(1, parts.shape[0]):
        total = total + parts[j, p]
    return total


def relax_kernel(source, inverse, first, parts, relaxed):
    for p in range(source.shape[0]):
        image = column_sum(parts, p)
        relaxed[p] = first[p] + omega * product(source[p] - image, inverse[p])


def residual_kernel(source, parts, weights, labels, residual, tentative):
    pblocks, nrhs, width = source.shape
    total = jnp.zeros((nrhs, pblocks * width), f32)
    for p in range(pblocks):
        value = source[p] - column_sum(parts, p)
        residual[p] = value
        weighted = value * weights[p : p + 1, :]
        aggregate = lax.broadcasted_iota(jnp.int32, (pblocks * width, width), 0)
        member = (aggregate == labels[p : p + 1, :]).astype(f32).astype(bf16)
        high, rest = split(weighted)
        low = (weighted - high.astype(f32) - rest.astype(f32)).astype(bf16)
        stacked = jnp.concatenate([high, rest, low, low], axis=0)
        spreadsum = lax.dot_general(
            stacked, member, (((1,), (1,)), ((), ())), preferred_element_type=f32
        )
        total = total + (
            spreadsum[:nrhs]
            + (spreadsum[nrhs : 2 * nrhs] + spreadsum[2 * nrhs : 3 * nrhs])
        )
    for p in range(pblocks):
        tentative[p] = total[:, p * width : (p + 1) * width]


def sum_kernel(parts, out):
    for p in range(out.shape[0]):
        out[p] = column_sum(parts, p)


def save_kernel(value, out):
    out[...] = value[...]


def tile_kernel(core, count, rows, cols, own, other, tiles, start, out):
    nout = out.shape[0]
    nsource = own.shape[0]
    live_count = count[0]
    mine = core[0]
    if start is None:
        out[...] = jnp.zeros_like(out)
    else:
        out[...] = start[...]

    def group(g, carry):
        terms = []
        for u in range(unroll):
            slot = g * unroll + u
            live = slot < live_count
            target = jnp.clip(cols[slot], 0, 2 * nsource - 1)
            index = (target // 4) * 2 + target % 2
            same = (target // 2) % 2 == mine
            x = jnp.where(same, own[index], other[index])
            x = jnp.where(live, x, 0.0)
            terms.append((jnp.clip(rows[slot], 0, nout - 1), product(x, tiles[slot])))
        for row, term in terms:
            out[row] = out[row] + term
        return carry

    lax.fori_loop(0, (live_count + unroll - 1) // unroll, group, 0)


def vmem(n):
    return [pl.BlockSpec(memory_space=pltpu.VMEM)] * n


def smem(n):
    return [pl.BlockSpec(memory_space=pltpu.SMEM)] * n


def call(kernel, shapes, *args):
    return pl.pallas_call(
        kernel,
        out_shape=tuple(jax.ShapeDtypeStruct(s, f32) for s in shapes),
        in_specs=vmem(len(args)),
        out_specs=tuple(vmem(len(shapes))),
        compiler_params=pltpu.CompilerParams(vmem_limit_bytes=grant),
    )(*args)


def tile_terms(core, count, rows, cols, own, other, tiles, start, nout):
    block = own.shape[1:]
    extra = () if start is None else (start,)

    def kernel(core, count, rows, cols, own, other, tiles, *rest):
        tile_kernel(core, count, rows, cols, own, other, tiles,
                    None if start is None else rest[0], rest[-1])

    return pl.pallas_call(
        kernel,
        out_shape=jax.ShapeDtypeStruct((nout,) + block, f32),
        in_specs=smem(4) + vmem(3 + len(extra)),
        out_specs=pl.BlockSpec(memory_space=pltpu.VMEM),
        compiler_params=pltpu.CompilerParams(vmem_limit_bytes=grant),
    )(core, count, rows, cols, own, other, tiles, *extra)


def pairs(v, axis):
    v = lax.all_gather(v, axis, axis=0, tiled=True, axis_index_groups=[[0, 1], [2, 3]])
    v = lax.optimization_barrier(v)
    return lax.all_gather(v, axis, axis=0, tiled=True, axis_index_groups=[[1, 2], [0, 3]])


def fan(v, axis):
    n = lax.axis_size(axis)
    v = lax.optimization_barrier(jnp.broadcast_to(v[None], (n,) + v.shape))
    return lax.all_to_all(v, axis, 0, 0, tiled=True)


def gather_rows(value):
    block = value.shape
    planes = fan(pairs(value[None], "zh"), "y")
    own = lax.optimization_barrier(planes.reshape((-1,) + block[1:]))
    other = lax.ppermute(own, "core", [(0, 1), (1, 0)])
    return own, other


def sum_columns(partial, pblocks):
    chunks = partial.reshape((-1, pblocks) + partial.shape[1:])
    return lax.all_to_all(chunks, ("zl", "x"), 0, 0, tiled=True)


def body(
    forcing_terms,
    diagonal_reciprocal,
    stiffness_submatrix,
    stiffness_source_index,
    stiffness_target_index,
    stiffness_nonzero_tally,
    interpolant_submatrix,
    interpolant_cluster_index,
    interpolant_target_index,
    interpolant_nonzero_tally,
    provisional_interpolant,
    cluster_label,
):
    source = forcing_terms[0, 0]
    inverse = diagonal_reciprocal[0, 0]
    tiles = stiffness_submatrix[0, 0]
    rows = stiffness_source_index[0, 0]
    cols = stiffness_target_index[0, 0]
    count = stiffness_nonzero_tally[0]
    core = lax.axis_index("core").astype(jnp.int32).reshape(1)
    pblocks = source.shape[0]
    ncol = lax.axis_size(("zl", "x"))
    block = source.shape

    first = pl.pallas_call(
        first_kernel,
        out_shape=jax.ShapeDtypeStruct(block, f32),
        in_specs=[pl.BlockSpec(memory_space=pltpu.MemorySpace.HBM)] * 2,
        out_specs=pl.BlockSpec(memory_space=pltpu.VMEM),
        scratch_shapes=[
            pltpu.VMEM(block, f32),
            pltpu.VMEM(inverse.shape, f32),
            pltpu.SemaphoreType.DMA((2,)),
        ],
        compiler_params=pltpu.CompilerParams(vmem_limit_bytes=grant),
        name="first",
    )(
        pltpu.with_memory_space_constraint(source, pltpu.MemorySpace.HBM),
        pltpu.with_memory_space_constraint(inverse, pltpu.MemorySpace.HBM),
    )
    own, other = gather_rows(first)
    partial = tile_terms(core, count, rows, cols, own, other, tiles, None, ncol * pblocks)
    parts = sum_columns(partial, pblocks)
    (relaxed,) = call(relax_kernel, (block,), source, inverse, first, parts)
    own, other = gather_rows(relaxed)
    partial = tile_terms(core, count, rows, cols, own, other, tiles, None, ncol * pblocks)
    parts = sum_columns(partial, pblocks)
    residual, tentative = call(
        residual_kernel,
        (block, block),
        source,
        parts,
        provisional_interpolant[0, 0],
        cluster_label[0, 0],
    )
    own, other = gather_rows(residual)
    share = tile_terms(
        core,
        interpolant_nonzero_tally[0],
        interpolant_cluster_index[0, 0],
        interpolant_target_index[0, 0],
        own,
        other,
        interpolant_submatrix[0, 0],
        tentative,
        pblocks,
    )
    shares = fan(share, "x")
    (share,) = call(sum_kernel, (block,), shares)
    shares = fan(share, "zl")
    (coarse,) = call(sum_kernel, (block,), shares)
    (relaxed,) = call(save_kernel, (block,), relaxed)
    (residual,) = call(save_kernel, (block,), residual)
    return (relaxed[None, None], residual[None, None], coarse[None])


def solution(mesh):
    grid = Mesh(mesh.devices.reshape(4, 4, 2, 4, 4), ("y", "zh", "core", "zl", "x"))
    row = ("y", "zh", "core")
    col = ("zl", "x")
    spec = P(row, col)

    return jax.shard_map(
        body,
        mesh=grid,
        in_specs=(spec,) * 12,
        out_specs=(spec, spec, P(row)),
        check_vma=False,
    )
```

```python
import jax
import jax.numpy as jnp
from jax import lax
from jax.experimental import pallas as pl
from jax.experimental.pallas import tpu as pltpu
from jax.sharding import Mesh, PartitionSpec as P


omega = 0.7
unroll = 16
grant = 16 * 2**20
f32 = jnp.float32
bf16 = jnp.bfloat16


def split(v):
    high = v.astype(bf16)
    return high, (v - high.astype(f32)).astype(bf16)


def product(x, w):
    n, m = x.shape[0], w.shape[1]
    left = jnp.concatenate(split(x), axis=0)
    right = jnp.concatenate(split(w), axis=1)
    full = jnp.dot(left, right, preferred_element_type=f32)
    small = full[:n, m:] + full[n:, :m] + full[n:, m:]
    return full[:n, :m] + small


def first_kernel(source_in, inverse_in, first, source, inverse, done):
    arrivals = [
        pltpu.make_async_copy(inverse_in, inverse, done.at[0]),
        pltpu.make_async_copy(source_in, source, done.at[1]),
    ]
    for arrival in arrivals:
        arrival.start()
    for arrival in arrivals:
        arrival.wait()
    for p in range(source.shape[0]):
        first[p] = omega * product(source[p], inverse[p])


def column_sum(parts, p):
    total = parts[0, p]
    for j in range(1, parts.shape[0]):
        total = total + parts[j, p]
    return total


def relax_kernel(source, inverse, first, parts, relaxed):
    for p in range(source.shape[0]):
        image = column_sum(parts, p)
        relaxed[p] = first[p] + omega * product(source[p] - image, inverse[p])


def residual_kernel(source, parts, weights, labels, residual, tentative):
    pblocks, nrhs, width = source.shape
    total = jnp.zeros((nrhs, pblocks * width), f32)
    for p in range(pblocks):
        value = source[p] - column_sum(parts, p)
        residual[p] = value
        weighted = value * weights[p : p + 1, :]
        aggregate = lax.broadcasted_iota(jnp.int32, (pblocks * width, width), 0)
        member = (aggregate == labels[p : p + 1, :]).astype(f32).astype(bf16)
        high, rest = split(weighted)
        low = (weighted - high.astype(f32) - rest.astype(f32)).astype(bf16)
        stacked = jnp.concatenate([high, rest, low, low], axis=0)
        spreadsum = lax.dot_general(
            stacked, member, (((1,), (1,)), ((), ())), preferred_element_type=f32
        )
        total = total + (
            spreadsum[:nrhs]
            + (spreadsum[nrhs : 2 * nrhs] + spreadsum[2 * nrhs : 3 * nrhs])
        )
    for p in range(pblocks):
        tentative[p] = total[:, p * width : (p + 1) * width]


def sum_kernel(parts, out):
    for p in range(out.shape[0]):
        out[p] = column_sum(parts, p)


def save_kernel(value, out):
    out[...] = value[...]


def tile_kernel(core, count, rows, cols, own, other, tiles, start, out):
    nout = out.shape[0]
    nsource = own.shape[0]
    capacity = tiles.shape[0]
    live_count = count[0]
    mine = core[0]
    if start is None:
        out[...] = jnp.zeros_like(out)
    else:
        out[...] = start[...]

    width = min(unroll, capacity)

    def group(g, carry):
        terms = []
        for u in range(width):
            slot = g * width + u
            live = slot < live_count
            target = cols[slot] & (2 * nsource - 1)
            index = ((target >> 2) << 1) | (target & 1)
            same = ((target >> 1) & 1) == mine
            x = jnp.where(same, own[index], other[index])
            x = jnp.where(live, x, 0.0)
            terms.append((rows[slot] & (nout - 1), product(x, tiles[slot])))
        for row, term in terms:
            out[row] = out[row] + term
        return carry

    group(0, 0)
    if capacity > width:

        @pl.when(live_count > width)
        def _():
            group(1, 0)


def vmem(n):
    return [pl.BlockSpec(memory_space=pltpu.VMEM)] * n


def smem(n):
    return [pl.BlockSpec(memory_space=pltpu.SMEM)] * n


def call(kernel, shapes, *args):
    return pl.pallas_call(
        kernel,
        out_shape=tuple(jax.ShapeDtypeStruct(s, f32) for s in shapes),
        in_specs=vmem(len(args)),
        out_specs=tuple(vmem(len(shapes))),
        compiler_params=pltpu.CompilerParams(vmem_limit_bytes=grant),
    )(*args)


def tile_terms(core, count, rows, cols, own, other, tiles, start, nout):
    block = own.shape[1:]
    extra = () if start is None else (start,)

    def kernel(core, count, rows, cols, own, other, tiles, *rest):
        tile_kernel(core, count, rows, cols, own, other, tiles,
                    None if start is None else rest[0], rest[-1])

    return pl.pallas_call(
        kernel,
        out_shape=jax.ShapeDtypeStruct((nout,) + block, f32),
        in_specs=smem(4) + vmem(3 + len(extra)),
        out_specs=pl.BlockSpec(memory_space=pltpu.VMEM),
        compiler_params=pltpu.CompilerParams(vmem_limit_bytes=grant),
    )(core, count, rows, cols, own, other, tiles, *extra)


def pairs(v, axis):
    v = lax.all_gather(v, axis, axis=0, tiled=True, axis_index_groups=[[0, 1], [2, 3]])
    v = lax.optimization_barrier(v)
    return lax.all_gather(v, axis, axis=0, tiled=True, axis_index_groups=[[1, 2], [0, 3]])


def fan(v, axis):
    n = lax.axis_size(axis)
    v = lax.optimization_barrier(jnp.broadcast_to(v[None], (n,) + v.shape))
    return lax.all_to_all(v, axis, 0, 0, tiled=True)


def gather_rows(value):
    block = value.shape
    planes = fan(pairs(value[None], "zh"), "y")
    own = lax.optimization_barrier(planes.reshape((-1,) + block[1:]))
    other = lax.ppermute(own, "core", [(0, 1), (1, 0)])
    return own, other


def sum_columns(partial, pblocks):
    chunks = partial.reshape((-1, pblocks) + partial.shape[1:])
    return lax.all_to_all(chunks, ("zl", "x"), 0, 0, tiled=True)


def body(
    forcing_terms,
    diagonal_reciprocal,
    stiffness_submatrix,
    stiffness_source_index,
    stiffness_target_index,
    stiffness_nonzero_tally,
    interpolant_submatrix,
    interpolant_cluster_index,
    interpolant_target_index,
    interpolant_nonzero_tally,
    provisional_interpolant,
    cluster_label,
):
    source = forcing_terms[0, 0]
    inverse = diagonal_reciprocal[0, 0]
    tiles = stiffness_submatrix[0, 0]
    rows = stiffness_source_index[0, 0]
    cols = stiffness_target_index[0, 0]
    count = stiffness_nonzero_tally[0]
    core = lax.axis_index("core").astype(jnp.int32).reshape(1)
    pblocks = source.shape[0]
    ncol = lax.axis_size(("zl", "x"))
    block = source.shape

    first = pl.pallas_call(
        first_kernel,
        out_shape=jax.ShapeDtypeStruct(block, f32),
        in_specs=[pl.BlockSpec(memory_space=pltpu.MemorySpace.HBM)] * 2,
        out_specs=pl.BlockSpec(memory_space=pltpu.VMEM),
        scratch_shapes=[
            pltpu.VMEM(block, f32),
            pltpu.VMEM(inverse.shape, f32),
            pltpu.SemaphoreType.DMA((2,)),
        ],
        compiler_params=pltpu.CompilerParams(vmem_limit_bytes=grant),
        name="first",
    )(
        pltpu.with_memory_space_constraint(source, pltpu.MemorySpace.HBM),
        pltpu.with_memory_space_constraint(inverse, pltpu.MemorySpace.HBM),
    )
    own, other = gather_rows(first)
    partial = tile_terms(core, count, rows, cols, own, other, tiles, None, ncol * pblocks)
    parts = sum_columns(partial, pblocks)
    (relaxed,) = call(relax_kernel, (block,), source, inverse, first, parts)
    own, other = gather_rows(relaxed)
    partial = tile_terms(core, count, rows, cols, own, other, tiles, None, ncol * pblocks)
    parts = sum_columns(partial, pblocks)
    residual, tentative = call(
        residual_kernel,
        (block, block),
        source,
        parts,
        provisional_interpolant[0, 0],
        cluster_label[0, 0],
    )
    own, other = gather_rows(residual)
    share = tile_terms(
        core,
        interpolant_nonzero_tally[0],
        interpolant_cluster_index[0, 0],
        interpolant_target_index[0, 0],
        own,
        other,
        interpolant_submatrix[0, 0],
        tentative,
        pblocks,
    )
    shares = fan(share, "x")
    (share,) = call(sum_kernel, (block,), shares)
    shares = fan(share, "zl")
    (coarse,) = call(sum_kernel, (block,), shares)
    (relaxed,) = call(save_kernel, (block,), relaxed)
    (residual,) = call(save_kernel, (block,), residual)
    return (relaxed[None, None], residual[None, None], coarse[None])


def solution(mesh):
    grid = Mesh(mesh.devices.reshape(4, 4, 2, 4, 4), ("y", "zh", "core", "zl", "x"))
    row = ("y", "zh", "core")
    col = ("zl", "x")
    spec = P(row, col)

    return jax.shard_map(
        body,
        mesh=grid,
        in_specs=(spec,) * 12,
        out_specs=(spec, spec, P(row)),
        check_vma=False,
    )
```

```python
import jax
import jax.numpy as jnp
from jax import lax
from jax.experimental import pallas as pl
from jax.experimental.pallas import tpu as pltpu
from jax.sharding import Mesh, PartitionSpec as P


omega = 0.7
unroll = 16
grant = 16 * 2**20
f32 = jnp.float32
bf16 = jnp.bfloat16


def split(v):
    high = v.astype(bf16)
    return high, (v - high.astype(f32)).astype(bf16)


def product(x, w):
    n, m = x.shape[0], w.shape[1]
    left = jnp.concatenate(split(x), axis=0)
    right = jnp.concatenate(split(w), axis=1)
    full = jnp.dot(left, right, preferred_element_type=f32)
    small = full[:n, m:] + full[n:, :m] + full[n:, m:]
    return full[:n, :m] + small


def first_kernel(source_in, inverse_in, first, source, inverse, done):
    arrivals = []
    for p in range(source.shape[0]):
        arrivals.append(
            (
                pltpu.make_async_copy(inverse_in.at[p], inverse.at[p], done.at[2 * p]),
                pltpu.make_async_copy(source_in.at[p], source.at[p], done.at[2 * p + 1]),
            )
        )
    for pair in arrivals:
        for arrival in pair:
            arrival.start()
    for p in range(source.shape[0]):
        for arrival in arrivals[p]:
            arrival.wait()
        first[p] = omega * product(source[p], inverse[p])


def column_sum(parts, p):
    total = parts[0, p]
    for j in range(1, parts.shape[0]):
        total = total + parts[j, p]
    return total


def relax_kernel(source, inverse, first, parts, relaxed):
    for p in range(source.shape[0]):
        image = column_sum(parts, p)
        relaxed[p] = first[p] + omega * product(source[p] - image, inverse[p])


def residual_kernel(source, parts, weights, labels, residual, tentative):
    pblocks, nrhs, width = source.shape
    total = jnp.zeros((nrhs, pblocks * width), f32)
    for p in range(pblocks):
        value = source[p] - column_sum(parts, p)
        residual[p] = value
        weighted = value * weights[p : p + 1, :]
        aggregate = lax.broadcasted_iota(jnp.int32, (pblocks * width, width), 0)
        member = (aggregate == labels[p : p + 1, :]).astype(f32).astype(bf16)
        high, rest = split(weighted)
        low = (weighted - high.astype(f32) - rest.astype(f32)).astype(bf16)
        stacked = jnp.concatenate([high, rest, low, low], axis=0)
        spreadsum = lax.dot_general(
            stacked, member, (((1,), (1,)), ((), ())), preferred_element_type=f32
        )
        total = total + (
            spreadsum[:nrhs]
            + (spreadsum[nrhs : 2 * nrhs] + spreadsum[2 * nrhs : 3 * nrhs])
        )
    for p in range(pblocks):
        tentative[p] = total[:, p * width : (p + 1) * width]


def sum_kernel(parts, out):
    for p in range(out.shape[0]):
        out[p] = column_sum(parts, p)


def save_kernel(value, out):
    out[...] = value[...]


def tile_kernel(core, count, rows, cols, own, other, tiles, start, out):
    nout = out.shape[0]
    nsource = own.shape[0]
    capacity = tiles.shape[0]
    live_count = count[0]
    mine = core[0]
    if start is None:
        out[...] = jnp.zeros_like(out)
    else:
        out[...] = start[...]

    width = min(unroll, capacity)

    def group(g, carry):
        terms = []
        for u in range(width):
            slot = g * width + u
            live = slot < live_count
            target = cols[slot] & (2 * nsource - 1)
            index = ((target >> 2) << 1) | (target & 1)
            same = ((target >> 1) & 1) == mine
            x = jnp.where(same, own[index], other[index])
            x = jnp.where(live, x, 0.0)
            terms.append((rows[slot] & (nout - 1), product(x, tiles[slot])))
        for row, term in terms:
            out[row] = out[row] + term
        return carry

    group(0, 0)
    if capacity > width:

        @pl.when(live_count > width)
        def _():
            group(1, 0)


def vmem(n):
    return [pl.BlockSpec(memory_space=pltpu.VMEM)] * n


def smem(n):
    return [pl.BlockSpec(memory_space=pltpu.SMEM)] * n


def call(kernel, shapes, *args):
    return pl.pallas_call(
        kernel,
        out_shape=tuple(jax.ShapeDtypeStruct(s, f32) for s in shapes),
        in_specs=vmem(len(args)),
        out_specs=tuple(vmem(len(shapes))),
        compiler_params=pltpu.CompilerParams(vmem_limit_bytes=grant),
    )(*args)


def tile_terms(core, count, rows, cols, own, other, tiles, start, nout):
    block = own.shape[1:]
    extra = () if start is None else (start,)

    def kernel(core, count, rows, cols, own, other, tiles, *rest):
        tile_kernel(core, count, rows, cols, own, other, tiles,
                    None if start is None else rest[0], rest[-1])

    return pl.pallas_call(
        kernel,
        out_shape=jax.ShapeDtypeStruct((nout,) + block, f32),
        in_specs=smem(4) + vmem(3 + len(extra)),
        out_specs=pl.BlockSpec(memory_space=pltpu.VMEM),
        compiler_params=pltpu.CompilerParams(vmem_limit_bytes=grant),
    )(core, count, rows, cols, own, other, tiles, *extra)


def pairs(v, axis):
    v = lax.all_gather(v, axis, axis=0, tiled=True, axis_index_groups=[[0, 1], [2, 3]])
    v = lax.optimization_barrier(v)
    return lax.all_gather(v, axis, axis=0, tiled=True, axis_index_groups=[[1, 2], [0, 3]])


def fan(v, axis):
    n = lax.axis_size(axis)
    v = lax.optimization_barrier(jnp.broadcast_to(v[None], (n,) + v.shape))
    return lax.all_to_all(v, axis, 0, 0, tiled=True)


def gather_rows(value):
    block = value.shape
    planes = fan(pairs(value[None], "zh"), "y")
    own = lax.optimization_barrier(planes.reshape((-1,) + block[1:]))
    other = lax.ppermute(own, "core", [(0, 1), (1, 0)])
    return own, other


def sum_columns(partial, pblocks):
    chunks = partial.reshape((-1, pblocks) + partial.shape[1:])
    return lax.all_to_all(chunks, ("zl", "x"), 0, 0, tiled=True)


def body(
    forcing_terms,
    diagonal_reciprocal,
    stiffness_submatrix,
    stiffness_source_index,
    stiffness_target_index,
    stiffness_nonzero_tally,
    interpolant_submatrix,
    interpolant_cluster_index,
    interpolant_target_index,
    interpolant_nonzero_tally,
    provisional_interpolant,
    cluster_label,
):
    source = forcing_terms[0, 0]
    inverse = diagonal_reciprocal[0, 0]
    tiles = stiffness_submatrix[0, 0]
    rows = stiffness_source_index[0, 0]
    cols = stiffness_target_index[0, 0]
    count = stiffness_nonzero_tally[0]
    core = lax.axis_index("core").astype(jnp.int32).reshape(1)
    pblocks = source.shape[0]
    ncol = lax.axis_size(("zl", "x"))
    block = source.shape

    first = pl.pallas_call(
        first_kernel,
        out_shape=jax.ShapeDtypeStruct(block, f32),
        in_specs=[pl.BlockSpec(memory_space=pltpu.MemorySpace.HBM)] * 2,
        out_specs=pl.BlockSpec(memory_space=pltpu.VMEM),
        scratch_shapes=[
            pltpu.VMEM(block, f32),
            pltpu.VMEM(inverse.shape, f32),
            pltpu.SemaphoreType.DMA((2 * block[0],)),
        ],
        compiler_params=pltpu.CompilerParams(vmem_limit_bytes=grant),
        name="first",
    )(
        pltpu.with_memory_space_constraint(source, pltpu.MemorySpace.HBM),
        pltpu.with_memory_space_constraint(inverse, pltpu.MemorySpace.HBM),
    )
    own, other = gather_rows(first)
    partial = tile_terms(core, count, rows, cols, own, other, tiles, None, ncol * pblocks)
    parts = sum_columns(partial, pblocks)
    (relaxed,) = call(relax_kernel, (block,), source, inverse, first, parts)
    own, other = gather_rows(relaxed)
    partial = tile_terms(core, count, rows, cols, own, other, tiles, None, ncol * pblocks)
    parts = sum_columns(partial, pblocks)
    residual, tentative = call(
        residual_kernel,
        (block, block),
        source,
        parts,
        provisional_interpolant[0, 0],
        cluster_label[0, 0],
    )
    own, other = gather_rows(residual)
    share = tile_terms(
        core,
        interpolant_nonzero_tally[0],
        interpolant_cluster_index[0, 0],
        interpolant_target_index[0, 0],
        own,
        other,
        interpolant_submatrix[0, 0],
        tentative,
        pblocks,
    )
    shares = fan(share, "x")
    (share,) = call(sum_kernel, (block,), shares)
    shares = fan(share, "zl")
    (coarse,) = call(sum_kernel, (block,), shares)
    (relaxed,) = call(save_kernel, (block,), relaxed)
    (residual,) = call(save_kernel, (block,), residual)
    return (relaxed[None, None], residual[None, None], coarse[None])


def solution(mesh):
    grid = Mesh(mesh.devices.reshape(4, 4, 2, 4, 4), ("y", "zh", "core", "zl", "x"))
    row = ("y", "zh", "core")
    col = ("zl", "x")
    spec = P(row, col)

    return jax.shard_map(
        body,
        mesh=grid,
        in_specs=(spec,) * 12,
        out_specs=(spec, spec, P(row)),
        check_vma=False,
    )
```

```python
import jax
import jax.numpy as jnp
from jax import lax
from jax.experimental import pallas as pl
from jax.experimental.pallas import tpu as pltpu
from jax.sharding import Mesh, PartitionSpec as P


omega = 0.7
unroll = 16
grant = 16 * 2**20
f32 = jnp.float32
bf16 = jnp.bfloat16


def split(v):
    high = v.astype(bf16)
    return high, (v - high.astype(f32)).astype(bf16)


def product(x, w):
    n, m = x.shape[0], w.shape[1]
    left = jnp.concatenate(split(x), axis=0)
    right = jnp.concatenate(split(w), axis=1)
    full = jnp.dot(left, right, preferred_element_type=f32)
    small = full[:n, m:] + full[n:, :m] + full[n:, m:]
    return full[:n, :m] + small


def first_kernel(source_in, inverse_in, first, source, inverse, done):
    arrivals = []
    for p in range(source.shape[0]):
        arrivals.append(
            (
                pltpu.make_async_copy(inverse_in.at[p], inverse.at[p], done.at[2 * p]),
                pltpu.make_async_copy(source_in.at[p], source.at[p], done.at[2 * p + 1]),
            )
        )
    for pair in arrivals:
        for arrival in pair:
            arrival.start()
    for p in range(source.shape[0]):
        for arrival in arrivals[p]:
            arrival.wait()
        first[p] = omega * product(source[p], inverse[p])


def column_sum(parts, p):
    total = parts[0, p]
    for j in range(1, parts.shape[0]):
        total = total + parts[j, p]
    return total


def relax_kernel(source, inverse, first, parts, relaxed):
    for p in range(source.shape[0]):
        image = column_sum(parts, p)
        relaxed[p] = first[p] + omega * product(source[p] - image, inverse[p])


def residual_kernel(source, parts, weights, labels, residual, tentative):
    pblocks, nrhs, width = source.shape
    total = jnp.zeros((nrhs, pblocks * width), f32)
    for p in range(pblocks):
        value = source[p] - column_sum(parts, p)
        residual[p] = value
        weighted = value * weights[p : p + 1, :]
        aggregate = lax.broadcasted_iota(jnp.int32, (pblocks * width, width), 0)
        member = (aggregate == labels[p : p + 1, :]).astype(f32).astype(bf16)
        high, rest = split(weighted)
        low = (weighted - high.astype(f32) - rest.astype(f32)).astype(bf16)
        stacked = jnp.concatenate([high, rest, low, low], axis=0)
        spreadsum = lax.dot_general(
            stacked, member, (((1,), (1,)), ((), ())), preferred_element_type=f32
        )
        total = total + (
            spreadsum[:nrhs]
            + (spreadsum[nrhs : 2 * nrhs] + spreadsum[2 * nrhs : 3 * nrhs])
        )
    for p in range(pblocks):
        tentative[p] = total[:, p * width : (p + 1) * width]


def sum_kernel(parts, out):
    for p in range(out.shape[0]):
        out[p] = column_sum(parts, p)


def save_kernel(value, out):
    out[...] = value[...]


def tile_kernel(core, count, rows, cols, own, other, tiles, start, out):
    nout = out.shape[0]
    nsource = own.shape[0]
    capacity = tiles.shape[0]
    live_count = count[0]
    mine = core[0]
    if start is None:
        out[...] = jnp.zeros_like(out)
    else:
        out[...] = start[...]

    width = min(unroll, capacity)

    def group(g, carry):
        terms = []
        for u in range(width):
            slot = g * width + u
            live = slot < live_count
            target = cols[slot] & (2 * nsource - 1)
            plane = (0x78 >> (2 * ((target >> 2) & 3))) & 3
            index = ((target >> 4) << 3) | (plane << 1) | (target & 1)
            same = ((target >> 1) & 1) == mine
            x = jnp.where(same, own[index], other[index])
            x = jnp.where(live, x, 0.0)
            terms.append((rows[slot] & (nout - 1), product(x, tiles[slot])))
        for row, term in terms:
            out[row] = out[row] + term
        return carry

    group(0, 0)
    if capacity > width:

        @pl.when(live_count > width)
        def _():
            group(1, 0)


def vmem(n):
    return [pl.BlockSpec(memory_space=pltpu.VMEM)] * n


def smem(n):
    return [pl.BlockSpec(memory_space=pltpu.SMEM)] * n


def call(kernel, shapes, *args):
    return pl.pallas_call(
        kernel,
        out_shape=tuple(jax.ShapeDtypeStruct(s, f32) for s in shapes),
        in_specs=vmem(len(args)),
        out_specs=tuple(vmem(len(shapes))),
        compiler_params=pltpu.CompilerParams(vmem_limit_bytes=grant),
    )(*args)


def tile_terms(core, count, rows, cols, own, other, tiles, start, nout):
    block = own.shape[1:]
    extra = () if start is None else (start,)

    def kernel(core, count, rows, cols, own, other, tiles, *rest):
        tile_kernel(core, count, rows, cols, own, other, tiles,
                    None if start is None else rest[0], rest[-1])

    return pl.pallas_call(
        kernel,
        out_shape=jax.ShapeDtypeStruct((nout,) + block, f32),
        in_specs=smem(4) + vmem(3 + len(extra)),
        out_specs=pl.BlockSpec(memory_space=pltpu.VMEM),
        compiler_params=pltpu.CompilerParams(vmem_limit_bytes=grant),
    )(core, count, rows, cols, own, other, tiles, *extra)


def pairs(v, axis):
    v = lax.all_gather(v, axis, axis=0, tiled=True, axis_index_groups=[[1, 2], [0, 3]])
    v = lax.optimization_barrier(v)
    return lax.all_gather(v, axis, axis=0, tiled=True, axis_index_groups=[[0, 1], [3, 2]])


def fan(v, axis):
    n = lax.axis_size(axis)
    v = lax.optimization_barrier(jnp.broadcast_to(v[None], (n,) + v.shape))
    return lax.all_to_all(v, axis, 0, 0, tiled=True)


def gather_rows(value):
    block = value.shape
    planes = fan(pairs(value[None], "zh"), "y")
    own = lax.optimization_barrier(planes.reshape((-1,) + block[1:]))
    other = lax.ppermute(own, "core", [(0, 1), (1, 0)])
    return own, other


def sum_columns(partial, pblocks):
    chunks = partial.reshape((-1, pblocks) + partial.shape[1:])
    return lax.all_to_all(chunks, ("zl", "x"), 0, 0, tiled=True)


def body(
    forcing_terms,
    diagonal_reciprocal,
    stiffness_submatrix,
    stiffness_source_index,
    stiffness_target_index,
    stiffness_nonzero_tally,
    interpolant_submatrix,
    interpolant_cluster_index,
    interpolant_target_index,
    interpolant_nonzero_tally,
    provisional_interpolant,
    cluster_label,
):
    source = forcing_terms[0, 0]
    inverse = diagonal_reciprocal[0, 0]
    tiles = stiffness_submatrix[0, 0]
    rows = stiffness_source_index[0, 0]
    cols = stiffness_target_index[0, 0]
    count = stiffness_nonzero_tally[0]
    core = lax.axis_index("core").astype(jnp.int32).reshape(1)
    pblocks = source.shape[0]
    ncol = lax.axis_size(("zl", "x"))
    block = source.shape

    first = pl.pallas_call(
        first_kernel,
        out_shape=jax.ShapeDtypeStruct(block, f32),
        in_specs=[pl.BlockSpec(memory_space=pltpu.MemorySpace.HBM)] * 2,
        out_specs=pl.BlockSpec(memory_space=pltpu.VMEM),
        scratch_shapes=[
            pltpu.VMEM(block, f32),
            pltpu.VMEM(inverse.shape, f32),
            pltpu.SemaphoreType.DMA((2 * block[0],)),
        ],
        compiler_params=pltpu.CompilerParams(vmem_limit_bytes=grant),
        name="first",
    )(
        pltpu.with_memory_space_constraint(source, pltpu.MemorySpace.HBM),
        pltpu.with_memory_space_constraint(inverse, pltpu.MemorySpace.HBM),
    )
    own, other = gather_rows(first)
    partial = tile_terms(core, count, rows, cols, own, other, tiles, None, ncol * pblocks)
    parts = sum_columns(partial, pblocks)
    (relaxed,) = call(relax_kernel, (block,), source, inverse, first, parts)
    own, other = gather_rows(relaxed)
    partial = tile_terms(core, count, rows, cols, own, other, tiles, None, ncol * pblocks)
    parts = sum_columns(partial, pblocks)
    residual, tentative = call(
        residual_kernel,
        (block, block),
        source,
        parts,
        provisional_interpolant[0, 0],
        cluster_label[0, 0],
    )
    own, other = gather_rows(residual)
    share = tile_terms(
        core,
        interpolant_nonzero_tally[0],
        interpolant_cluster_index[0, 0],
        interpolant_target_index[0, 0],
        own,
        other,
        interpolant_submatrix[0, 0],
        tentative,
        pblocks,
    )
    shares = fan(share, "x")
    (share,) = call(sum_kernel, (block,), shares)
    shares = fan(share, "zl")
    (coarse,) = call(sum_kernel, (block,), shares)
    (relaxed,) = call(save_kernel, (block,), relaxed)
    (residual,) = call(save_kernel, (block,), residual)
    return (relaxed[None, None], residual[None, None], coarse[None])


def solution(mesh):
    grid = Mesh(mesh.devices.reshape(4, 4, 2, 4, 4), ("y", "zh", "core", "zl", "x"))
    row = ("y", "zh", "core")
    col = ("zl", "x")
    spec = P(row, col)

    return jax.shard_map(
        body,
        mesh=grid,
        in_specs=(spec,) * 12,
        out_specs=(spec, spec, P(row)),
        check_vma=False,
    )
```
